32 devices in a mesh: blk: 16 (over z, y, core), rep: 2 (over x).
Axes of the slice: x: 2, y: 2, z: 4, core: 2. Of those that a mesh axis runs over, the one named last changes fastest.
Arguments:
- features: bfloat16 [16384, 256], P('blk'), may hold values from -6 to 6
- weight_self: bfloat16 [256, 256], replicated, may hold values from -0.375 to 0.375
- weight_neighbor: bfloat16 [256, 256], replicated, may hold values from -0.375 to 0.375
- bias_vector: float32 [256], replicated, may hold values from -3 to 3
- tile_row: int32 [16, 16, 64], P('blk', 'rep'), may hold values from 0 to 7
- tile_column: int32 [16, 16, 64], P('blk', 'rep'), may hold values from 0 to 7
- tile_value: int32 [16, 16, 64], P('blk', 'rep'), may hold values from 0 to 127
- tile_count: int32 [16, 16], P('blk', 'rep'), may hold values from 16 to 64
- tile_table: bfloat16 [4096, 128, 128], P(('blk', 'rep')), may hold values from -0.0625 to 0.0625
- cotangent: bfloat16 [16384, 256], P('blk'), may hold values from -6 to 6
Outputs:
- activations: bfloat16 [16384, 256], P('blk')
- grad_features: bfloat16 [16384, 256], P('blk')
- grad_weight_self: float32 [256, 256], replicated
- grad_weight_neighbor: float32 [256, 256], replicated
- grad_bias: float32 [256], replicated
The draws below stay inside these ranges and needn't reach their ends.
All inputs are finite; a program needn't handle non-finite values.
Results may differ from the reference program's by a relative error of at most 0.025.
Values may be sent and summed in bfloat16 or wider, within the bound.
A program may use at most 64 MiB of HBM per device.

```python
import jax
import jax.numpy as jnp
from jax import lax

F = 256
TILE = 128
R_DEV = 1024
SLOTS = 64
VALS = 128
BLOCKS_DEV = 8
GROUPS = 16
STEPS = 16
NODES = 16384
TABLE_TILES = 4096
N_BLK = 16
N_REP = 2


def draw_tile_count(key, part):
    step_ids = jnp.arange(STEPS, dtype=jnp.int32)
    distance = jnp.minimum(step_ids, STEPS - step_ids)
    drawn = jax.random.randint(key, (GROUPS, STEPS), SLOTS // 4, SLOTS // 2 + 1, dtype=jnp.int32)
    return jnp.where(distance[None, :] <= 1, SLOTS, drawn).astype(jnp.int32)


def touch_ends(entries, key, low, top_value):
    extent = entries.shape
    place = [jax.random.randint(jax.random.fold_in(key, axis), (), 0, extent[axis]) for axis in range(len(extent))]
    entries = entries.at[tuple(place)].set(low)
    longest = extent.index(max(extent))
    place[longest] = (place[longest] + 1) % extent[longest]
    return entries.at[tuple(place)].set(top_value)


def steps_of(rng, extent, split, smallest, high):
    gain = 1.0
    for dim, blocks in split:
        draws = jax.random.uniform(jax.random.fold_in(jax.random.fold_in(rng, 6), dim), (blocks,), jnp.float32, smallest / len(split), high / len(split))
        gain = gain * jnp.repeat(jnp.exp(draws), extent[dim] // blocks).reshape((-1,) + (1,) * (len(extent) - 1 - dim))
    return gain


def scatter_about(own_key, extent, width, bound, pieces=(), kind=jnp.bfloat16):
    gain = steps_of(own_key, extent, pieces, -0.22, 0.18) if pieces else 1.0
    result = jax.random.normal(own_key, extent, jnp.float32) * width * gain
    return jnp.minimum(jnp.maximum(result, -bound), bound).astype(kind)


def setup_inputs(seed: int = 0) -> dict:
    streams_of = jax.random.split(jax.random.key(seed), 11)
    features = scatter_about(streams_of[0], (NODES, F), 1.0, 6.0, ((0, 16),))
    weight_self = scatter_about(streams_of[1], (F, F), F ** -0.5, 0.375)
    weight_neighbor = scatter_about(streams_of[2], (F, F), F ** -0.5, 0.375)
    bias_vector = scatter_about(streams_of[3], (F,), 0.5, 3.0, (), jnp.float32)
    tile_row = touch_ends(jax.random.randint(streams_of[4], (GROUPS, STEPS, SLOTS), 0, BLOCKS_DEV), jax.random.fold_in(streams_of[4], 1), 0, BLOCKS_DEV - 1).astype(jnp.int32)
    tile_column = touch_ends(jax.random.randint(streams_of[5], (GROUPS, STEPS, SLOTS), 0, BLOCKS_DEV), jax.random.fold_in(streams_of[5], 1), 0, BLOCKS_DEV - 1).astype(jnp.int32)
    tile_value = touch_ends(jax.random.randint(streams_of[6], (GROUPS, STEPS, SLOTS), 0, VALS), jax.random.fold_in(streams_of[6], 1), 0, VALS - 1).astype(jnp.int32)
    tile_count = draw_tile_count(jax.random.fold_in(streams_of[10], 71), 0)
    tile_table = scatter_about(streams_of[8], (TABLE_TILES, TILE, TILE), (TILE * SLOTS * STEPS * TILE // (2 * R_DEV)) ** -0.5, 0.0625, ((0, 32),))
    cotangent = scatter_about(streams_of[9], (NODES, F), 1.0, 6.0, ((0, 16),))
    return dict(features=features, weight_self=weight_self, weight_neighbor=weight_neighbor, bias_vector=bias_vector, tile_row=tile_row, tile_column=tile_column, tile_value=tile_value, tile_count=tile_count, tile_table=tile_table, cotangent=cotangent)


def reference(features, weight_self, weight_neighbor, bias_vector, tile_row, tile_column, tile_value, tile_count, tile_table, cotangent):
    block_count = R_DEV // TILE
    step_count = N_BLK // N_REP
    step_ids = jnp.arange(N_BLK, dtype=jnp.int32)
    slot_index = jnp.arange(SLOTS, dtype=jnp.int32)
    block_index = jnp.arange(block_count, dtype=jnp.int32)
    value_table = tile_table.astype(jnp.float32)
    source_blocks = features.astype(jnp.float32).reshape(N_BLK, block_count, TILE, F)

    def lists_of(group_id):
        table_base = (group_id * N_REP + step_ids // step_count) * VALS
        tile_values = value_table[table_base[:, None] + tile_value[group_id]]
        is_live = slot_index[None, :] < tile_count[group_id][:, None]
        rows_hit = ((tile_row[group_id][..., None] == block_index) & is_live[..., None]).astype(jnp.float32)
        columns_hit = ((tile_column[group_id][..., None] == block_index) & is_live[..., None]).astype(jnp.float32)
        partner = ((group_id - step_ids) % N_BLK).astype(jnp.int32)
        return tile_values, rows_hit, columns_hit, partner

    def forward_group(group_id):
        tile_values, rows_hit, columns_hit, partner = lists_of(group_id)
        picked = source_blocks[partner[:, None], tile_column[group_id]]
        products = jnp.einsum("skab,skbf->skaf", tile_values, picked)
        return jnp.einsum("skr,skaf->raf", rows_hit, products)

    aggregate = lax.map(forward_group, step_ids)
    aggregate_b = aggregate.reshape(NODES, F).astype(jnp.bfloat16)
    before = jnp.dot(features, weight_self, preferred_element_type=jnp.float32)
    before = before + jnp.dot(aggregate_b, weight_neighbor, preferred_element_type=jnp.float32) + bias_vector
    sigmoid_pre = jax.nn.sigmoid(before)
    activations = (before * sigmoid_pre).astype(jnp.bfloat16)
    derivative = sigmoid_pre * (1.0 + before * (1.0 - sigmoid_pre))
    grad_pre = (cotangent.astype(jnp.float32) * derivative).astype(jnp.bfloat16)
    grad_weight_self = jnp.dot(features.T, grad_pre, preferred_element_type=jnp.float32)
    grad_weight_neighbor = jnp.dot(aggregate_b.T, grad_pre, preferred_element_type=jnp.float32)
    grad_bias = jnp.sum(grad_pre.astype(jnp.float32), axis=0)
    self_term = jnp.dot(grad_pre, weight_self.T, preferred_element_type=jnp.float32)
    sent_back = jnp.dot(grad_pre, weight_neighbor.T, preferred_element_type=jnp.float32).astype(jnp.bfloat16)
    sent_blocks = sent_back.astype(jnp.float32).reshape(N_BLK, block_count, TILE, F)

    def backward_group(running, group_id):
        tile_values, rows_hit, columns_hit, partner = lists_of(group_id)
        picked = sent_blocks[group_id][tile_row[group_id]]
        products = jnp.einsum("skab,skaf->skbf", tile_values, picked)
        addition = jnp.einsum("skc,skbf->scbf", columns_hit, products)
        return running.at[partner].add(addition), None

    pushed, unused = lax.scan(backward_group, jnp.zeros((N_BLK, block_count, TILE, F), jnp.float32), step_ids)
    grad_features = (self_term + pushed.reshape(NODES, F)).astype(jnp.bfloat16)
    return activations, grad_features, grad_weight_self, grad_weight_neighbor, grad_bias
```

```python
import functools

import jax
import jax.numpy as jnp
from jax import lax
from jax.experimental import pallas as pl
from jax.experimental.pallas import tpu as pltpu
from jax.sharding import PartitionSpec as P

ROWS_ROWS = (((0,), (0,)), ((), ()))
COLS_COLS = (((1,), (1,)), ((), ()))


def build_kernel(rows, columns, values, counts, table, dense):
    step = pl.program_id(0)
    tile = table.shape[1]
    dense[...] = jnp.zeros_like(dense)

    def add_tile(slot, carry):
        row = pl.multiple_of(rows[step, slot] * tile, tile)
        column = pl.multiple_of(columns[step, slot] * tile, tile)
        place = (0, pl.ds(row, tile), pl.ds(column, tile))
        dense[place] = dense[place] + table[values[step, slot]]
        return carry

    lax.fori_loop(0, counts[step], add_tile, 0)


def build_dense(rows, columns, values, counts, table, row_total):
    step_count = rows.shape[0]
    return pl.pallas_call(
        build_kernel,
        grid_spec=pltpu.PrefetchScalarGridSpec(
            num_scalar_prefetch=4,
            grid=(step_count,),
            in_specs=[pl.BlockSpec(table.shape, lambda s, *_: (0, 0, 0))],
            out_specs=pl.BlockSpec((1, row_total, row_total), lambda s, *_: (s, 0, 0)),
        ),
        out_shape=jax.ShapeDtypeStruct((step_count, row_total, row_total), jnp.bfloat16),
        cost_estimate=pl.CostEstimate(
            flops=0, bytes_accessed=20 * 2**20, transcendentals=0
        ),
        name="build",
    )(rows, columns, values, counts, table)


def forward_kernel(sources, dense, panel, out, total):
    step = pl.program_id(0)
    term = jnp.dot(dense[0], panel[0], preferred_element_type=jnp.float32)

    @pl.when(step == 0)
    def _():
        total[...] = term

    @pl.when(step > 0)
    def _():
        total[...] += term

    @pl.when(step == pl.num_programs(0) - 1)
    def _():
        out[...] = total[...].astype(out.dtype)


def forward(sources, dense, panels):
    step_count, row_total, _ = dense.shape
    width = panels.shape[2]
    return pl.pallas_call(
        forward_kernel,
        grid_spec=pltpu.PrefetchScalarGridSpec(
            num_scalar_prefetch=1,
            grid=(step_count,),
            in_specs=[
                pl.BlockSpec((1, row_total, row_total), lambda s, src: (s, 0, 0)),
                pl.BlockSpec((1, row_total, width), lambda s, src: (src[s], 0, 0)),
            ],
            out_specs=pl.BlockSpec((row_total, width), lambda s, src: (0, 0)),
            scratch_shapes=[pltpu.VMEM((row_total, width), jnp.float32)],
        ),
        out_shape=jax.ShapeDtypeStruct((row_total, width), jnp.bfloat16),
        name="forward",
    )(sources, dense, panels)


def layer_kernel(
    features, mine, other, weight_self, weight_neighbor, bias, cotangent,
    activations, sent_t, self_t, grads,
):
    f32 = jnp.float32
    width = features.shape[1]
    aggregate = (mine[...].astype(f32) + other[...].astype(f32)).astype(jnp.bfloat16)
    pre = (
        jnp.dot(features[...], weight_self[...], preferred_element_type=f32)
        + jnp.dot(aggregate, weight_neighbor[...], preferred_element_type=f32)
        + bias[...]
    )
    sigmoid = jax.nn.sigmoid(pre)
    activations[...] = (pre * sigmoid).astype(activations.dtype)
    derivative = sigmoid * (1.0 + pre * (1.0 - sigmoid))
    grad_pre = (cotangent[...].astype(f32) * derivative).astype(jnp.bfloat16)
    sent_t[...] = lax.dot_general(
        weight_neighbor[...], grad_pre, COLS_COLS, preferred_element_type=f32
    ).astype(sent_t.dtype)
    self_t[...] = lax.dot_general(
        weight_self[...], grad_pre, COLS_COLS, preferred_element_type=f32
    )
    grads[0:width, :] = lax.dot_general(
        features[...], grad_pre, ROWS_ROWS, preferred_element_type=f32
    ).astype(grads.dtype)
    grads[width : 2 * width, :] = lax.dot_general(
        aggregate, grad_pre, ROWS_ROWS, preferred_element_type=f32
    ).astype(grads.dtype)
    summed = jnp.sum(grad_pre.astype(f32), axis=0, keepdims=True)
    tail = grads.shape[0] - 2 * width
    grads[2 * width :, :] = jnp.broadcast_to(summed, (tail, width)).astype(grads.dtype)


def layer(features, mine, other, weight_self, weight_neighbor, bias, cotangent):
    row_total, width = features.shape
    shape = jax.ShapeDtypeStruct
    return pl.pallas_call(
        layer_kernel,
        out_shape=(
            shape((row_total, width), jnp.bfloat16),
            shape((width, row_total), jnp.bfloat16),
            shape((width, row_total), jnp.float32),
            shape((2 * width + 32, width), jnp.bfloat16),
        ),
        name="layer",
    )(features, mine, other, weight_self, weight_neighbor, bias, cotangent)


def backward_kernel(step_count, targets, dense, sent_t, out):
    step = pl.program_id(0)

    @pl.when(step < step_count)
    def _():
        out[0] = jnp.dot(
            sent_t[...], dense[0], preferred_element_type=jnp.float32
        ).astype(out.dtype)

    @pl.when(step >= step_count)
    def _():
        out[...] = jnp.zeros_like(out)


def backward(targets, dense, sent_t):
    step_count, row_total, _ = dense.shape
    width = sent_t.shape[0]
    cycle = targets.shape[0]
    return pl.pallas_call(
        functools.partial(backward_kernel, step_count),
        grid_spec=pltpu.PrefetchScalarGridSpec(
            num_scalar_prefetch=1,
            grid=(cycle,),
            in_specs=[
                pl.BlockSpec(
                    (1, row_total, row_total),
                    lambda s, dst: (jnp.minimum(s, step_count - 1), 0, 0),
                ),
                pl.BlockSpec((width, row_total), lambda s, dst: (0, 0)),
            ],
            out_specs=pl.BlockSpec((1, width, row_total), lambda s, dst: (dst[s], 0, 0)),
        ),
        out_shape=jax.ShapeDtypeStruct((cycle, width, row_total), jnp.bfloat16),
        name="backward",
    )(targets, dense, sent_t)


def on_device(
    features,
    weight_self,
    weight_neighbor,
    bias_vector,
    tile_row,
    tile_column,
    tile_value,
    tile_count,
    tile_table,
    cotangent,
):
    f32, bf16 = jnp.float32, jnp.bfloat16
    cycle_length = lax.axis_size("blk")
    replicas = lax.axis_size("rep")
    step_count = cycle_length // replicas
    group = lax.axis_index("blk")
    replica = lax.axis_index("rep")
    row_total, width = features.shape

    panels = lax.all_gather(features, "blk")
    dense = build_dense(
        tile_row[0], tile_column[0], tile_value[0], tile_count[0], tile_table, row_total
    )
    reached = jnp.mod(
        group - replica * step_count - jnp.arange(cycle_length, dtype=jnp.int32),
        cycle_length,
    ).astype(jnp.int32)
    mine = forward(reached[:step_count], dense, panels)
    bit = 1
    while True:
        other = lax.ppermute(mine, "rep", [(i, i ^ bit) for i in range(replicas)])
        bit *= 2
        if bit >= replicas:
            break
        mine = (mine.astype(f32) + other.astype(f32)).astype(bf16)
    activations, sent_t, self_t, grads = layer(
        features, mine, other, weight_self, weight_neighbor,
        bias_vector.reshape(1, width), cotangent,
    )
    partial = backward(reached, dense, sent_t)
    pushed = lax.psum_scatter(partial, "blk", scatter_dimension=0)
    grads = lax.psum(grads, "blk").astype(f32)
    bit = 1
    while bit < replicas:
        other = lax.ppermute(pushed, "rep", [(i, i ^ bit) for i in range(replicas)])
        pushed = (pushed.astype(f32) + other.astype(f32)).astype(
            bf16 if 2 * bit < replicas else f32
        )
        bit *= 2
    grad_features = (self_t + pushed).astype(bf16).T
    return (
        activations,
        grad_features,
        grads[:width],
        grads[width : 2 * width],
        grads[2 * width],
    )


def solution(mesh):
    placed = (
        P("blk", None),
        P(),
        P(),
        P(),
        P("blk", "rep", None),
        P("blk", "rep", None),
        P("blk", "rep", None),
        P("blk", "rep"),
        P(("blk", "rep"), None, None),
        P("blk", None),
    )
    return jax.shard_map(
        on_device,
        mesh=mesh,
        in_specs=placed,
        out_specs=(P("blk", None), P("blk", None), P(), P(), P()),
        check_vma=False,
    )
```

```python
import functools

import jax
import jax.numpy as jnp
from jax import lax
from jax.experimental import pallas as pl
from jax.experimental.pallas import tpu as pltpu
from jax.sharding import PartitionSpec as P

ROWS_ROWS = (((0,), (0,)), ((), ()))
COLS_COLS = (((1,), (1,)), ((), ()))


def build_kernel(rows, columns, values, counts, table, dense):
    step = pl.program_id(0)
    tile = table.shape[1]
    dense[...] = jnp.zeros_like(dense)

    def add_tile(slot, carry):
        row = pl.multiple_of(rows[step, slot] * tile, tile)
        column = pl.multiple_of(columns[step, slot] * tile, tile)
        place = (0, pl.ds(row, tile), pl.ds(column, tile))
        dense[place] = dense[place] + table[values[step, slot]]
        return carry

    lax.fori_loop(0, counts[step], add_tile, 0)


def build_dense(rows, columns, values, counts, table, row_total):
    step_count = rows.shape[0]
    return pl.pallas_call(
        build_kernel,
        grid_spec=pltpu.PrefetchScalarGridSpec(
            num_scalar_prefetch=4,
            grid=(step_count,),
            in_specs=[pl.BlockSpec(table.shape, lambda s, *_: (0, 0, 0))],
            out_specs=pl.BlockSpec((1, row_total, row_total), lambda s, *_: (s, 0, 0)),
        ),
        out_shape=jax.ShapeDtypeStruct((step_count, row_total, row_total), jnp.bfloat16),
        cost_estimate=pl.CostEstimate(
            flops=0, bytes_accessed=20 * 2**20, transcendentals=0
        ),
        name="build",
    )(rows, columns, values, counts, table)


def ring_place(cycle, replicas):
    group = lax.axis_index("blk")
    replica = lax.axis_index("rep")
    reverse = (2 * replica) // replicas if replicas > 1 else 0 * replica
    ahead = lax.rem(group + 1 - 2 * reverse + cycle, cycle)
    behind = lax.rem(group - 1 + 2 * reverse + cycle, cycle)
    return group, replica, reverse, ahead, behind


def greet(devices):
    barrier = pltpu.get_barrier_semaphore()
    for device in devices:
        pl.semaphore_signal(
            barrier, inc=1, device_id={"blk": device},
            device_id_type=pl.DeviceIdType.MESH,
        )
    pl.semaphore_wait(barrier, len(devices))


def forward_kernel(
    cycle, replicas, pieces, features, dense, out,
    slots, blocks, total, block_sem, first_sem, send_sem, recv_sem,
):
    steps, rows = blocks.shape[0], blocks.shape[1]
    _, _, reverse, ahead, behind = ring_place(cycle, replicas)
    size = rows // pieces
    first = pltpu.make_async_copy(features, slots.at[0], first_sem)
    first.start()

    def load(step):
        return pltpu.make_async_copy(
            dense.at[step], blocks.at[step], block_sem.at[step]
        )

    def in_order(hop):
        return hop * (1 - reverse) + (steps - hop) * reverse

    @pl.loop(0, steps)
    def _(hop):
        load(in_order(hop + reverse)).start()

    greet((ahead, behind))
    first.wait()

    def hop_copy(hop, piece):
        span = pl.ds(piece * size, size)
        return pltpu.make_async_remote_copy(
            src_ref=slots.at[hop, span],
            dst_ref=slots.at[hop + 1, span],
            send_sem=send_sem.at[hop, piece],
            recv_sem=recv_sem.at[hop, piece],
            device_id={"blk": ahead},
            device_id_type=pl.DeviceIdType.MESH,
        )

    total[...] = jnp.zeros_like(total)
    hops = steps - 1 + reverse

    @pl.loop(0, hops + 1)
    def _(hop):
        for piece in range(pieces):
            @pl.when(hop > 0)
            def _():
                hop_copy(hop - 1, piece).wait_recv()

            @pl.when(hop < hops)
            def _():
                hop_copy(hop, piece).start()

        step = in_order(hop)

        @pl.when(step < steps)
        def _():
            load(step).wait()
            total[...] += jnp.dot(
                blocks[step], slots[hop], preferred_element_type=jnp.float32
            )

    out[...] = total[...].astype(out.dtype)

    @pl.loop(0, hops)
    def _(hop):
        for piece in range(pieces):
            hop_copy(hop, piece).wait_send()


def forward(cycle, replicas, features, dense):
    step_count, row_total, _ = dense.shape
    width = features.shape[1]
    pieces = 4
    return pl.pallas_call(
        functools.partial(forward_kernel, cycle, replicas, pieces),
        in_specs=[pl.BlockSpec(memory_space=pl.ANY)] * 2,
        out_specs=pl.BlockSpec(memory_space=pltpu.VMEM),
        out_shape=jax.ShapeDtypeStruct((row_total, width), jnp.bfloat16),
        scratch_shapes=[
            pltpu.VMEM((step_count + 1, row_total, width), jnp.bfloat16),
            pltpu.VMEM(dense.shape, jnp.bfloat16),
            pltpu.VMEM((row_total, width), jnp.float32),
            pltpu.SemaphoreType.DMA((step_count,)),
            pltpu.SemaphoreType.DMA,
            pltpu.SemaphoreType.DMA((step_count, pieces)),
            pltpu.SemaphoreType.DMA((step_count, pieces)),
        ],
        compiler_params=pltpu.CompilerParams(collective_id=0, has_side_effects=True),
        name="forward",
    )(features, dense)


def layer_kernel(
    features, mine, other, weight_self, weight_neighbor, bias, cotangent,
    activations, sent_t, self_t, grads,
):
    f32 = jnp.float32
    width = features.shape[1]
    aggregate = (mine[...].astype(f32) + other[...].astype(f32)).astype(jnp.bfloat16)
    pre = (
        jnp.dot(features[...], weight_self[...], preferred_element_type=f32)
        + jnp.dot(aggregate, weight_neighbor[...], preferred_element_type=f32)
        + bias[...]
    )
    sigmoid = jax.nn.sigmoid(pre)
    activations[...] = (pre * sigmoid).astype(activations.dtype)
    derivative = sigmoid * (1.0 + pre * (1.0 - sigmoid))
    grad_pre = (cotangent[...].astype(f32) * derivative).astype(jnp.bfloat16)
    sent_t[...] = lax.dot_general(
        weight_neighbor[...], grad_pre, COLS_COLS, preferred_element_type=f32
    ).astype(sent_t.dtype)
    self_t[...] = lax.dot_general(
        weight_self[...], grad_pre, COLS_COLS, preferred_element_type=f32
    )
    grad_self = lax.dot_general(
        features[...], grad_pre, ROWS_ROWS, preferred_element_type=f32
    ).astype(grads.dtype)
    grad_neighbor = lax.dot_general(
        aggregate, grad_pre, ROWS_ROWS, preferred_element_type=f32
    ).astype(grads.dtype)
    summed = jnp.sum(grad_pre.astype(f32), axis=0, keepdims=True)
    parts = grads.shape[0]
    depth = 2 * width // parts
    tail = grads.shape[1] - depth
    bias_rows = jnp.broadcast_to(summed, (tail, width)).astype(grads.dtype)
    for part in range(parts):
        source, place = (
            (grad_self, part) if 2 * part < parts else (grad_neighbor, part - parts // 2)
        )
        grads[part, 0:depth, :] = source[place * depth : (place + 1) * depth, :]
        grads[part, depth:, :] = bias_rows


def layer(parts, features, mine, other, weight_self, weight_neighbor, bias, cotangent):
    row_total, width = features.shape
    shape = jax.ShapeDtypeStruct
    return pl.pallas_call(
        layer_kernel,
        out_shape=(
            shape((row_total, width), jnp.bfloat16),
            shape((width, row_total), jnp.bfloat16),
            shape((width, row_total), jnp.float32),
            shape((parts, 2 * width // parts + 16, width), jnp.bfloat16),
        ),
        name="layer",
    )(features, mine, other, weight_self, weight_neighbor, bias, cotangent)


def backward_kernel(
    cycle, replicas, pieces, sent_t, dense, grads, out, part_out,
    landed, held, part_landed, part_held, blocks, term,
    block_sem, send_sem, recv_sem,
):
    steps = blocks.shape[0]
    width = sent_t.shape[0]
    size = width // pieces
    f32 = jnp.float32
    group, replica, reverse, behind, ahead = ring_place(cycle, replicas)

    def load(step):
        return pltpu.make_async_copy(
            dense.at[step], blocks.at[step], block_sem.at[step]
        )

    def in_order(hop):
        return (steps - 1 - hop) * (1 - reverse) + hop * reverse

    @pl.loop(0, steps)
    def _(hop):
        load(in_order(hop)).start()

    greet((ahead, behind))

    def hop_copy(hop, piece):
        if piece < pieces:
            span = pl.ds(piece * size, size)
            source, target = held.at[hop, span], landed.at[hop, span]
        else:
            source, target = part_held.at[hop], part_landed.at[hop]
        return pltpu.make_async_remote_copy(
            src_ref=source,
            dst_ref=target,
            send_sem=send_sem.at[hop, piece],
            recv_sem=recv_sem.at[hop, piece],
            device_id={"blk": ahead},
            device_id_type=pl.DeviceIdType.MESH,
        )

    hops = steps - 1 + reverse

    @pl.loop(0, steps)
    def _(hop):
        step = in_order(hop)
        target = lax.rem(group - steps * replica - step + 2 * cycle, cycle)
        load(step).wait()
        term[...] = jnp.dot(sent_t[...], blocks[step], preferred_element_type=f32)
        for piece in range(pieces + 1):
            span = pl.ds(piece * size, size)

            @pl.when(hop > 0)
            def _():
                hop_copy(hop - 1, piece).wait_recv()
                if piece < pieces:
                    held[hop, span] = (
                        term[span] + landed[hop - 1, span].astype(f32)
                    ).astype(held.dtype)
                else:
                    part_held[hop] = (
                        grads[target].astype(f32) + part_landed[hop - 1].astype(f32)
                    ).astype(part_held.dtype)

            @pl.when(hop == 0)
            def _():
                if piece < pieces:
                    held[hop, span] = term[span].astype(held.dtype)
                else:
                    part_held[hop] = grads[target]

            @pl.when(hop < hops)
            def _():
                hop_copy(hop, piece).start()

    @pl.when(reverse == 0)
    def _():
        out[...] = held[steps - 1]
        part_out[...] = part_held[steps - 1]

    @pl.when(reverse == 1)
    def _():
        for piece in range(pieces + 1):
            hop_copy(steps - 1, piece).wait_recv()
        out[...] = landed[steps - 1]
        part_out[...] = part_landed[steps - 1]

    @pl.loop(0, hops)
    def _(hop):
        for piece in range(pieces + 1):
            hop_copy(hop, piece).wait_send()


def backward(cycle, replicas, sent_t, dense, grads):
    step_count, row_total, _ = dense.shape
    width = sent_t.shape[0]
    part = grads.shape[1:]
    pieces = 4
    bf16 = jnp.bfloat16
    return pl.pallas_call(
        functools.partial(backward_kernel, cycle, replicas, pieces),
        in_specs=[
            pl.BlockSpec(memory_space=pltpu.VMEM),
            pl.BlockSpec(memory_space=pl.ANY),
            pl.BlockSpec(memory_space=pltpu.VMEM),
        ],
        out_specs=[pl.BlockSpec(memory_space=pltpu.VMEM)] * 2,
        out_shape=(
            jax.ShapeDtypeStruct((width, row_total), bf16),
            jax.ShapeDtypeStruct(part, bf16),
        ),
        scratch_shapes=[
            pltpu.VMEM((step_count, width, row_total), bf16),
            pltpu.VMEM((step_count, width, row_total), bf16),
            pltpu.VMEM((step_count, *part), bf16),
            pltpu.VMEM((step_count, *part), bf16),
            pltpu.VMEM(dense.shape, bf16),
            pltpu.VMEM((width, row_total), jnp.float32),
            pltpu.SemaphoreType.DMA((step_count,)),
            pltpu.SemaphoreType.DMA((step_count, pieces + 1)),
            pltpu.SemaphoreType.DMA((step_count, pieces + 1)),
        ],
        compiler_params=pltpu.CompilerParams(collective_id=1, has_side_effects=True),
        name="backward",
    )(sent_t, dense, grads)


def spread_kernel(cycle, part, out, gathered, own_sem, send_sem, recv_sem):
    group = lax.axis_index("blk")
    greet([lax.rem(group + away, cycle) for away in range(1, cycle)])
    own = pltpu.make_async_copy(part, gathered.at[group], own_sem)
    own.start()

    def put(away):
        return pltpu.make_async_remote_copy(
            src_ref=part,
            dst_ref=gathered.at[group],
            send_sem=send_sem.at[away],
            recv_sem=recv_sem.at[away],
            device_id={"blk": lax.rem(group + away, cycle)},
            device_id_type=pl.DeviceIdType.MESH,
        )

    @pl.loop(1, cycle)
    def _(away):
        put(away).start()

    own.wait()

    @pl.loop(1, cycle)
    def _(away):
        put(away).wait()

    out[...] = gathered[...].astype(out.dtype)


def spread(cycle, part):
    return pl.pallas_call(
        functools.partial(spread_kernel, cycle),
        in_specs=[pl.BlockSpec(memory_space=pltpu.VMEM)],
        out_specs=pl.BlockSpec(memory_space=pltpu.VMEM),
        out_shape=jax.ShapeDtypeStruct((cycle, *part.shape), jnp.float32),
        scratch_shapes=[
            pltpu.VMEM((cycle, *part.shape), part.dtype),
            pltpu.SemaphoreType.DMA,
            pltpu.SemaphoreType.DMA((cycle,)),
            pltpu.SemaphoreType.DMA((cycle,)),
        ],
        compiler_params=pltpu.CompilerParams(collective_id=2, has_side_effects=True),
        name="spread",
    )(part)


def on_device(
    features,
    weight_self,
    weight_neighbor,
    bias_vector,
    tile_row,
    tile_column,
    tile_value,
    tile_count,
    tile_table,
    cotangent,
):
    f32, bf16 = jnp.float32, jnp.bfloat16
    cycle_length = lax.axis_size("blk")
    replicas = lax.axis_size("rep")
    step_count = cycle_length // replicas
    replica = lax.axis_index("rep")
    row_total, width = features.shape

    jump = jnp.minimum(replica, replicas - 1 - replica)
    jump_bits = max(replicas // 2 - 1, 0).bit_length()
    reverse = (2 * replica) // replicas

    def shifted(array, sign):
        for bit in range(jump_bits):
            by = sign * (step_count << bit)
            moved = jnp.where(
                reverse == 0,
                lax.ppermute(
                    array, "blk",
                    [(i, (i + by) % cycle_length) for i in range(cycle_length)],
                ),
                lax.ppermute(
                    array, "blk",
                    [(i, (i - by) % cycle_length) for i in range(cycle_length)],
                ),
            )
            array = jnp.where(jump // (1 << bit) % 2 == 1, moved, array)
        return array

    dense = build_dense(
        tile_row[0], tile_column[0], tile_value[0], tile_count[0], tile_table, row_total
    )
    mine = forward(cycle_length, replicas, shifted(features, 1), dense)
    bit = 1
    while True:
        other = lax.ppermute(mine, "rep", [(i, i ^ bit) for i in range(replicas)])
        bit *= 2
        if bit >= replicas:
            break
        mine = (mine.astype(f32) + other.astype(f32)).astype(bf16)
    activations, sent_t, self_t, grads = layer(
        cycle_length, features, mine, other, weight_self, weight_neighbor,
        bias_vector.reshape(1, width), cotangent,
    )
    pushed, part = backward(cycle_length, replicas, sent_t, dense, grads)
    pushed, part = shifted(pushed, -1), shifted(part, -1)

    def over_replicas(array):
        bit = 1
        while bit < replicas:
            other = lax.ppermute(array, "rep", [(i, i ^ bit) for i in range(replicas)])
            array = array.astype(f32) + other.astype(f32)
            bit *= 2
            if bit < replicas:
                array = array.astype(bf16)
        return array

    part = over_replicas(part)
    depth = 2 * width // cycle_length
    weights = spread(cycle_length, part[:depth].astype(bf16))
    weights = weights.reshape(2 * width, width)
    pushed = over_replicas(pushed)
    grad_features = (self_t + pushed).astype(bf16).T
    return (
        activations,
        grad_features,
        weights[:width],
        weights[width:],
        part[depth].astype(f32),
    )


def solution(mesh):
    placed = (
        P("blk", None),
        P(),
        P(),
        P(),
        P("blk", "rep", None),
        P("blk", "rep", None),
        P("blk", "rep", None),
        P("blk", "rep"),
        P(("blk", "rep"), None, None),
        P("blk", None),
    )
    return jax.shard_map(
        on_device,
        mesh=mesh,
        in_specs=placed,
        out_specs=(P("blk", None), P("blk", None), P(), P(), P()),
        check_vma=False,
    )
```

```python
import functools

import jax
import jax.numpy as jnp
from jax import lax
from jax.experimental import pallas as pl
from jax.experimental.pallas import tpu as pltpu
from jax.sharding import PartitionSpec as P

ROWS_ROWS = (((0,), (0,)), ((), ()))
COLS_COLS = (((1,), (1,)), ((), ()))


def build_kernel(rows, columns, values, counts, table, dense):
    step = pl.program_id(0)
    tile = table.shape[1]
    dense[...] = jnp.zeros_like(dense)

    def add_tile(slot, carry):
        row = pl.multiple_of(rows[step, slot] * tile, tile)
        column = pl.multiple_of(columns[step, slot] * tile, tile)
        place = (0, pl.ds(row, tile), pl.ds(column, tile))
        dense[place] = dense[place] + table[values[step, slot]]
        return carry

    lax.fori_loop(0, counts[step], add_tile, 0)


def build_dense(rows, columns, values, counts, table, row_total):
    step_count = rows.shape[0]
    return pl.pallas_call(
        build_kernel,
        grid_spec=pltpu.PrefetchScalarGridSpec(
            num_scalar_prefetch=4,
            grid=(step_count,),
            in_specs=[pl.BlockSpec(table.shape, lambda s, *_: (0, 0, 0))],
            out_specs=pl.BlockSpec((1, row_total, row_total), lambda s, *_: (s, 0, 0)),
        ),
        out_shape=jax.ShapeDtypeStruct((step_count, row_total, row_total), jnp.bfloat16),
        cost_estimate=pl.CostEstimate(
            flops=0, bytes_accessed=20 * 2**20, transcendentals=0
        ),
        name="build",
    )(rows, columns, values, counts, table)


def ring_place(cycle, replicas):
    group = lax.axis_index("blk")
    replica = lax.axis_index("rep")
    reverse = (2 * replica) // replicas if replicas > 1 else 0 * replica
    ahead = lax.rem(group + 1 - 2 * reverse + cycle, cycle)
    behind = lax.rem(group - 1 + 2 * reverse + cycle, cycle)
    return group, replica, reverse, ahead, behind


def greet(devices):
    barrier = pltpu.get_barrier_semaphore()
    for device in devices:
        pl.semaphore_signal(
            barrier, inc=1, device_id={"blk": device},
            device_id_type=pl.DeviceIdType.MESH,
        )
    pl.semaphore_wait(barrier, len(devices))


def forward_kernel(
    cycle, replicas, pieces, features, dense, out,
    slots, blocks, total, block_sem, first_sem, send_sem, recv_sem,
):
    steps, rows = blocks.shape[0], blocks.shape[1]
    _, _, reverse, ahead, behind = ring_place(cycle, replicas)
    size = rows // pieces
    first = pltpu.make_async_copy(features, slots.at[0], first_sem)
    first.start()

    def load(step):
        return pltpu.make_async_copy(
            dense.at[step], blocks.at[step], block_sem.at[step]
        )

    def in_order(hop):
        return hop * (1 - reverse) + (steps - hop) * reverse

    @pl.loop(0, steps)
    def _(hop):
        load(in_order(hop + reverse)).start()

    greet((ahead, behind))
    first.wait()

    def hop_copy(hop, piece):
        span = pl.ds(piece * size, size)
        return pltpu.make_async_remote_copy(
            src_ref=slots.at[hop, span],
            dst_ref=slots.at[hop + 1, span],
            send_sem=send_sem.at[hop, piece],
            recv_sem=recv_sem.at[hop, piece],
            device_id={"blk": ahead},
            device_id_type=pl.DeviceIdType.MESH,
        )

    total[...] = jnp.zeros_like(total)
    hops = steps - 1 + reverse

    @pl.loop(0, hops + 1)
    def _(hop):
        for piece in range(pieces):
            @pl.when(hop > 0)
            def _():
                hop_copy(hop - 1, piece).wait_recv()

            @pl.when(hop < hops)
            def _():
                hop_copy(hop, piece).start()

        step = in_order(hop)

        @pl.when(step < steps)
        def _():
            load(step).wait()
            total[...] += jnp.dot(
                blocks[step], slots[hop], preferred_element_type=jnp.float32
            )

    out[...] = total[...].astype(out.dtype)

    @pl.loop(0, hops)
    def _(hop):
        for piece in range(pieces):
            hop_copy(hop, piece).wait_send()


LANES = 4
OVER_LAYERS, OVER_PAIR, OVER_CORE, RELAYED = range(4)


def layered_forward_kernel(
    cycle, replicas, pieces, features, dense, out,
    slots, blocks, total, block_sem, first_sem, send_sem, recv_sem,
):
    steps, rows = blocks.shape[0], blocks.shape[1]
    group, _, reverse, _, _ = ring_place(cycle, replicas)
    size = rows // pieces
    layer_id, lane = group // LANES, lax.rem(group, LANES)
    pair, core = lane // 2, lax.rem(lane, 2)
    along = LANES * (1 - 2 * reverse)
    ahead = lax.rem(group + along + cycle, cycle)
    behind = lax.rem(group - along + cycle, cycle)
    across = layer_id * LANES + (1 - pair) * 2 + core
    beside = layer_id * LANES + pair * 2 + 1 - core
    lane_across = (1 - pair) * 2 + core
    first = pltpu.make_async_copy(features, slots.at[0, lane], first_sem)
    first.start()

    def load(step):
        return pltpu.make_async_copy(
            dense.at[step], blocks.at[step], block_sem.at[step]
        )

    def in_order(hop):
        return hop * (1 - reverse) + (steps - 1 - hop) * reverse

    @pl.loop(0, steps)
    def _(hop):
        load(in_order(hop)).start()

    greet((ahead, behind, across, beside))
    first.wait()

    def copy(kind, distance, piece):
        span = pl.ds(piece * size, size)
        whose = lane_across if kind == RELAYED else lane
        landing = distance + 1 if kind == OVER_LAYERS else distance
        return pltpu.make_async_remote_copy(
            src_ref=slots.at[distance, whose, span],
            dst_ref=slots.at[landing, whose, span],
            send_sem=send_sem.at[kind, distance, piece],
            recv_sem=recv_sem.at[kind, distance, piece],
            device_id={"blk": {OVER_LAYERS: ahead, OVER_PAIR: across}.get(kind, beside)},
            device_id_type=pl.DeviceIdType.MESH,
        )

    def gives(distance):
        return {0: pair == reverse, 1: None, 2: pair != reverse}[distance]

    def gets(distance):
        return {0: pair != reverse, 1: None, 2: pair == reverse}[distance]

    def guarded(condition, act):
        if condition is None:
            act()
        else:
            pl.when(condition)(act)

    def give(distance, piece):
        if distance < 2:
            copy(OVER_LAYERS, distance, piece).start()
        guarded(gives(distance), lambda: copy(OVER_PAIR, distance, piece).start())
        copy(OVER_CORE, distance, piece).start()

    def relay(distance):
        def act():
            for piece in range(pieces):
                copy(OVER_PAIR, distance, piece).wait_recv()
                copy(RELAYED, distance, piece).start()

        guarded(gets(distance), act)

    def arrive(distance):
        for piece in range(pieces):
            copy(OVER_LAYERS, distance - 1, piece).wait_recv()
            give(distance, piece)

    def multiply(distance):
        for piece in range(pieces):
            copy(OVER_CORE, distance, piece).wait_recv()

        def act():
            for piece in range(pieces):
                copy(RELAYED, distance, piece).wait_recv()

        guarded(gets(distance), act)

        @pl.loop(0, steps)
        def _(hop):
            step = in_order(hop)
            away = hop + reverse
            source = lax.rem(lane + (2 * reverse - 1) * away + 2 * steps, LANES)
            far = ((LANES - 1 - lane) * (1 - reverse) + lane * reverse + away) // LANES

            @pl.when(far == distance)
            def _():
                load(step).wait()
                total[...] += jnp.dot(
                    blocks[step], slots[distance, source],
                    preferred_element_type=jnp.float32,
                )

    for piece in range(pieces):
        give(0, piece)
    total[...] = jnp.zeros_like(total)
    arrive(1)
    relay(0)
    multiply(0)
    relay(1)
    arrive(2)
    multiply(1)
    relay(2)
    multiply(2)
    out[...] = total[...].astype(out.dtype)
    for distance in range(3):
        for piece in range(pieces):
            if distance < 2:
                copy(OVER_LAYERS, distance, piece).wait_send()
            guarded(
                gives(distance),
                functools.partial(copy(OVER_PAIR, distance, piece).wait_send),
            )
            copy(OVER_CORE, distance, piece).wait_send()
            guarded(
                gets(distance),
                functools.partial(copy(RELAYED, distance, piece).wait_send),
            )


def forward(cycle, replicas, features, dense):
    step_count, row_total, _ = dense.shape
    width = features.shape[1]
    pieces = 4
    layered = step_count == 2 * LANES and cycle >= 3 * LANES and replicas == 2
    if layered:
        slots, sems = (3, LANES, row_total, width), (4, 3, pieces)
    else:
        slots, sems = (step_count + 1, row_total, width), (step_count, pieces)
    return pl.pallas_call(
        functools.partial(
            layered_forward_kernel if layered else forward_kernel,
            cycle, replicas, pieces,
        ),
        in_specs=[pl.BlockSpec(memory_space=pl.ANY)] * 2,
        out_specs=pl.BlockSpec(memory_space=pltpu.VMEM),
        out_shape=jax.ShapeDtypeStruct((row_total, width), jnp.bfloat16),
        scratch_shapes=[
            pltpu.VMEM(slots, jnp.bfloat16),
            pltpu.VMEM(dense.shape, jnp.bfloat16),
            pltpu.VMEM((row_total, width), jnp.float32),
            pltpu.SemaphoreType.DMA((step_count,)),
            pltpu.SemaphoreType.DMA,
            pltpu.SemaphoreType.DMA(sems),
            pltpu.SemaphoreType.DMA(sems),
        ],
        compiler_params=pltpu.CompilerParams(collective_id=0, has_side_effects=True),
        name="forward",
    )(features, dense)


def layer_kernel(
    features, mine, other, weight_self, weight_neighbor, bias, cotangent,
    activations, sent_t, self_t, grads,
):
    f32 = jnp.float32
    width = features.shape[1]
    aggregate = (mine[...].astype(f32) + other[...].astype(f32)).astype(jnp.bfloat16)
    pre = (
        jnp.dot(features[...], weight_self[...], preferred_element_type=f32)
        + jnp.dot(aggregate, weight_neighbor[...], preferred_element_type=f32)
        + bias[...]
    )
    sigmoid = jax.nn.sigmoid(pre)
    activations[...] = (pre * sigmoid).astype(activations.dtype)
    derivative = sigmoid * (1.0 + pre * (1.0 - sigmoid))
    grad_pre = (cotangent[...].astype(f32) * derivative).astype(jnp.bfloat16)
    sent_t[...] = lax.dot_general(
        weight_neighbor[...], grad_pre, COLS_COLS, preferred_element_type=f32
    ).astype(sent_t.dtype)
    self_t[...] = lax.dot_general(
        weight_self[...], grad_pre, COLS_COLS, preferred_element_type=f32
    )
    grad_self = lax.dot_general(
        features[...], grad_pre, ROWS_ROWS, preferred_element_type=f32
    ).astype(grads.dtype)
    grad_neighbor = lax.dot_general(
        aggregate, grad_pre, ROWS_ROWS, preferred_element_type=f32
    ).astype(grads.dtype)
    summed = jnp.sum(grad_pre.astype(f32), axis=0, keepdims=True)
    parts = grads.shape[0]
    depth = 2 * width // parts
    tail = grads.shape[1] - depth
    bias_rows = jnp.broadcast_to(summed, (tail, width)).astype(grads.dtype)
    for part in range(parts):
        source, place = (
            (grad_self, part) if 2 * part < parts else (grad_neighbor, part - parts // 2)
        )
        grads[part, 0:depth, :] = source[place * depth : (place + 1) * depth, :]
        grads[part, depth:, :] = bias_rows


def layer(parts, features, mine, other, weight_self, weight_neighbor, bias, cotangent):
    row_total, width = features.shape
    shape = jax.ShapeDtypeStruct
    return pl.pallas_call(
        layer_kernel,
        out_shape=(
            shape((row_total, width), jnp.bfloat16),
            shape((width, row_total), jnp.bfloat16),
            shape((width, row_total), jnp.float32),
            shape((parts, 2 * width // parts + 16, width), jnp.bfloat16),
        ),
        name="layer",
    )(features, mine, other, weight_self, weight_neighbor, bias, cotangent)


def backward_kernel(
    cycle, replicas, pieces, sent_t, dense, grads, out, part_out,
    landed, held, part_landed, part_held, blocks, term,
    block_sem, send_sem, recv_sem,
):
    steps = blocks.shape[0]
    width = sent_t.shape[0]
    size = width // pieces
    f32 = jnp.float32
    group, replica, reverse, behind, ahead = ring_place(cycle, replicas)

    def load(step):
        return pltpu.make_async_copy(
            dense.at[step], blocks.at[step], block_sem.at[step]
        )

    def in_order(hop):
        return (steps - 1 - hop) * (1 - reverse) + hop * reverse

    @pl.loop(0, steps)
    def _(hop):
        load(in_order(hop)).start()

    greet((ahead, behind))

    def hop_copy(hop, piece):
        if piece < pieces:
            span = pl.ds(piece * size, size)
            source, target = held.at[hop, span], landed.at[hop, span]
        else:
            source, target = part_held.at[hop], part_landed.at[hop]
        return pltpu.make_async_remote_copy(
            src_ref=source,
            dst_ref=target,
            send_sem=send_sem.at[hop, piece],
            recv_sem=recv_sem.at[hop, piece],
            device_id={"blk": ahead},
            device_id_type=pl.DeviceIdType.MESH,
        )

    hops = steps - 1 + reverse

    @pl.loop(0, steps)
    def _(hop):
        step = in_order(hop)
        target = lax.rem(group - steps * replica - step + 2 * cycle, cycle)
        load(step).wait()
        term[...] = jnp.dot(sent_t[...], blocks[step], preferred_element_type=f32)
        for piece in range(pieces + 1):
            span = pl.ds(piece * size, size)

            @pl.when(hop > 0)
            def _():
                hop_copy(hop - 1, piece).wait_recv()
                if piece < pieces:
                    held[hop, span] = (
                        term[span] + landed[hop - 1, span].astype(f32)
                    ).astype(held.dtype)
                else:
                    part_held[hop] = (
                        grads[target].astype(f32) + part_landed[hop - 1].astype(f32)
                    ).astype(part_held.dtype)

            @pl.when(hop == 0)
            def _():
                if piece < pieces:
                    held[hop, span] = term[span].astype(held.dtype)
                else:
                    part_held[hop] = grads[target]

            @pl.when(hop < hops)
            def _():
                hop_copy(hop, piece).start()

    @pl.when(reverse == 0)
    def _():
        out[...] = held[steps - 1]
        part_out[...] = part_held[steps - 1]

    @pl.when(reverse == 1)
    def _():
        for piece in range(pieces + 1):
            hop_copy(steps - 1, piece).wait_recv()
        out[...] = landed[steps - 1]
        part_out[...] = part_landed[steps - 1]

    @pl.loop(0, hops)
    def _(hop):
        for piece in range(pieces + 1):
            hop_copy(hop, piece).wait_send()


def backward(cycle, replicas, sent_t, dense, grads):
    step_count, row_total, _ = dense.shape
    width = sent_t.shape[0]
    part = grads.shape[1:]
    pieces = 4
    bf16 = jnp.bfloat16
    return pl.pallas_call(
        functools.partial(backward_kernel, cycle, replicas, pieces),
        in_specs=[
            pl.BlockSpec(memory_space=pltpu.VMEM),
            pl.BlockSpec(memory_space=pl.ANY),
            pl.BlockSpec(memory_space=pltpu.VMEM),
        ],
        out_specs=[pl.BlockSpec(memory_space=pltpu.VMEM)] * 2,
        out_shape=(
            jax.ShapeDtypeStruct((width, row_total), bf16),
            jax.ShapeDtypeStruct(part, bf16),
        ),
        scratch_shapes=[
            pltpu.VMEM((step_count, width, row_total), bf16),
            pltpu.VMEM((step_count, width, row_total), bf16),
            pltpu.VMEM((step_count, *part), bf16),
            pltpu.VMEM((step_count, *part), bf16),
            pltpu.VMEM(dense.shape, bf16),
            pltpu.VMEM((width, row_total), jnp.float32),
            pltpu.SemaphoreType.DMA((step_count,)),
            pltpu.SemaphoreType.DMA((step_count, pieces + 1)),
            pltpu.SemaphoreType.DMA((step_count, pieces + 1)),
        ],
        compiler_params=pltpu.CompilerParams(collective_id=1, has_side_effects=True),
        name="backward",
    )(sent_t, dense, grads)


def spread_kernel(cycle, part, out, gathered, own_sem, send_sem, recv_sem):
    group = lax.axis_index("blk")
    greet([lax.rem(group + away, cycle) for away in range(1, cycle)])
    own = pltpu.make_async_copy(part, gathered.at[group], own_sem)
    own.start()

    def put(away):
        return pltpu.make_async_remote_copy(
            src_ref=part,
            dst_ref=gathered.at[group],
            send_sem=send_sem.at[away],
            recv_sem=recv_sem.at[away],
            device_id={"blk": lax.rem(group + away, cycle)},
            device_id_type=pl.DeviceIdType.MESH,
        )

    @pl.loop(1, cycle)
    def _(away):
        put(away).start()

    own.wait()

    @pl.loop(1, cycle)
    def _(away):
        put(away).wait()

    out[...] = gathered[...].astype(out.dtype)


def spread(cycle, part):
    return pl.pallas_call(
        functools.partial(spread_kernel, cycle),
        in_specs=[pl.BlockSpec(memory_space=pltpu.VMEM)],
        out_specs=pl.BlockSpec(memory_space=pltpu.VMEM),
        out_shape=jax.ShapeDtypeStruct((cycle, *part.shape), jnp.float32),
        scratch_shapes=[
            pltpu.VMEM((cycle, *part.shape), part.dtype),
            pltpu.SemaphoreType.DMA,
            pltpu.SemaphoreType.DMA((cycle,)),
            pltpu.SemaphoreType.DMA((cycle,)),
        ],
        compiler_params=pltpu.CompilerParams(collective_id=2, has_side_effects=True),
        name="spread",
    )(part)


def on_device(
    features,
    weight_self,
    weight_neighbor,
    bias_vector,
    tile_row,
    tile_column,
    tile_value,
    tile_count,
    tile_table,
    cotangent,
):
    f32, bf16 = jnp.float32, jnp.bfloat16
    cycle_length = lax.axis_size("blk")
    replicas = lax.axis_size("rep")
    step_count = cycle_length // replicas
    replica = lax.axis_index("rep")
    row_total, width = features.shape

    jump = jnp.minimum(replica, replicas - 1 - replica)
    jump_bits = max(replicas // 2 - 1, 0).bit_length()
    reverse = (2 * replica) // replicas

    def shifted(array, sign):
        for bit in range(jump_bits):
            by = sign * (step_count << bit)
            moved = jnp.where(
                reverse == 0,
                lax.ppermute(
                    array, "blk",
                    [(i, (i + by) % cycle_length) for i in range(cycle_length)],
                ),
                lax.ppermute(
                    array, "blk",
                    [(i, (i - by) % cycle_length) for i in range(cycle_length)],
                ),
            )
            array = jnp.where(jump // (1 << bit) % 2 == 1, moved, array)
        return array

    dense = build_dense(
        tile_row[0], tile_column[0], tile_value[0], tile_count[0], tile_table, row_total
    )
    mine = forward(cycle_length, replicas, shifted(features, 1), dense)
    bit = 1
    while True:
        other = lax.ppermute(mine, "rep", [(i, i ^ bit) for i in range(replicas)])
        bit *= 2
        if bit >= replicas:
            break
        mine = (mine.astype(f32) + other.astype(f32)).astype(bf16)
    activations, sent_t, self_t, grads = layer(
        cycle_length, features, mine, other, weight_self, weight_neighbor,
        bias_vector.reshape(1, width), cotangent,
    )
    pushed, part = backward(cycle_length, replicas, sent_t, dense, grads)
    pushed, part = shifted(pushed, -1), shifted(part, -1)

    def over_replicas(array):
        bit = 1
        while bit < replicas:
            other = lax.ppermute(array, "rep", [(i, i ^ bit) for i in range(replicas)])
            array = array.astype(f32) + other.astype(f32)
            bit *= 2
            if bit < replicas:
                array = array.astype(bf16)
        return array

    part = over_replicas(part)
    depth = 2 * width // cycle_length
    weights = spread(cycle_length, part[:depth].astype(bf16))
    weights = weights.reshape(2 * width, width)
    pushed = over_replicas(pushed)
    grad_features = (self_t + pushed).astype(bf16).T
    return (
        activations,
        grad_features,
        weights[:width],
        weights[width:],
        part[depth].astype(f32),
    )


def solution(mesh):
    placed = (
        P("blk", None),
        P(),
        P(),
        P(),
        P("blk", "rep", None),
        P("blk", "rep", None),
        P("blk", "rep", None),
        P("blk", "rep"),
        P(("blk", "rep"), None, None),
        P("blk", None),
    )
    return jax.shard_map(
        on_device,
        mesh=mesh,
        in_specs=placed,
        out_specs=(P("blk", None), P("blk", None), P(), P(), P()),
        check_vma=False,
    )
```

```python
import functools

import jax
import jax.numpy as jnp
from jax import lax
from jax.experimental import pallas as pl
from jax.experimental.pallas import tpu as pltpu
from jax.sharding import PartitionSpec as P

ROWS_ROWS = (((0,), (0,)), ((), ()))
COLS_COLS = (((1,), (1,)), ((), ()))


def build_kernel(rows, columns, values, counts, table, dense):
    step = pl.program_id(0)
    tile = table.shape[1]
    dense[...] = jnp.zeros_like(dense)

    def add_tile(slot, carry):
        row = pl.multiple_of(rows[step, slot] * tile, tile)
        column = pl.multiple_of(columns[step, slot] * tile, tile)
        place = (0, pl.ds(row, tile), pl.ds(column, tile))
        dense[place] = dense[place] + table[values[step, slot]]
        return carry

    lax.fori_loop(0, counts[step], add_tile, 0)


def build_dense(rows, columns, values, counts, table, row_total):
    step_count = rows.shape[0]
    return pl.pallas_call(
        build_kernel,
        grid_spec=pltpu.PrefetchScalarGridSpec(
            num_scalar_prefetch=4,
            grid=(step_count,),
            in_specs=[pl.BlockSpec(table.shape, lambda s, *_: (0, 0, 0))],
            out_specs=pl.BlockSpec((1, row_total, row_total), lambda s, *_: (s, 0, 0)),
        ),
        out_shape=jax.ShapeDtypeStruct((step_count, row_total, row_total), jnp.bfloat16),
        cost_estimate=pl.CostEstimate(
            flops=0, bytes_accessed=20 * 2**20, transcendentals=0
        ),
        name="build",
    )(rows, columns, values, counts, table)


def ring_place(cycle, replicas):
    group = lax.axis_index("blk")
    replica = lax.axis_index("rep")
    reverse = (2 * replica) // replicas if replicas > 1 else 0 * replica
    ahead = lax.rem(group + 1 - 2 * reverse + cycle, cycle)
    behind = lax.rem(group - 1 + 2 * reverse + cycle, cycle)
    return group, replica, reverse, ahead, behind


def greet(devices):
    barrier = pltpu.get_barrier_semaphore()
    for device in devices:
        pl.semaphore_signal(
            barrier, inc=1, device_id={"blk": device},
            device_id_type=pl.DeviceIdType.MESH,
        )
    pl.semaphore_wait(barrier, len(devices))


def forward_kernel(
    cycle, replicas, pieces, features, dense, out,
    slots, blocks, total, block_sem, first_sem, send_sem, recv_sem,
):
    steps, rows = blocks.shape[0], blocks.shape[1]
    _, _, reverse, ahead, behind = ring_place(cycle, replicas)
    size = rows // pieces
    first = pltpu.make_async_copy(features, slots.at[0], first_sem)
    first.start()

    def load(step):
        return pltpu.make_async_copy(
            dense.at[step], blocks.at[step], block_sem.at[step]
        )

    def in_order(hop):
        return hop * (1 - reverse) + (steps - hop) * reverse

    @pl.loop(0, steps)
    def _(hop):
        load(in_order(hop + reverse)).start()

    greet((ahead, behind))
    first.wait()

    def hop_copy(hop, piece):
        span = pl.ds(piece * size, size)
        return pltpu.make_async_remote_copy(
            src_ref=slots.at[hop, span],
            dst_ref=slots.at[hop + 1, span],
            send_sem=send_sem.at[hop, piece],
            recv_sem=recv_sem.at[hop, piece],
            device_id={"blk": ahead},
            device_id_type=pl.DeviceIdType.MESH,
        )

    total[...] = jnp.zeros_like(total)
    hops = steps - 1 + reverse

    @pl.loop(0, hops + 1)
    def _(hop):
        for piece in range(pieces):
            @pl.when(hop > 0)
            def _():
                hop_copy(hop - 1, piece).wait_recv()

            @pl.when(hop < hops)
            def _():
                hop_copy(hop, piece).start()

        step = in_order(hop)

        @pl.when(step < steps)
        def _():
            load(step).wait()
            total[...] += jnp.dot(
                blocks[step], slots[hop], preferred_element_type=jnp.float32
            )

    out[...] = total[...].astype(out.dtype)

    @pl.loop(0, hops)
    def _(hop):
        for piece in range(pieces):
            hop_copy(hop, piece).wait_send()


LANES = 4
OVER_LAYERS, OVER_PAIR, OVER_CORE, RELAYED = range(4)


def layered_forward_kernel(
    cycle, replicas, pieces, features, dense, out,
    slots, blocks, total, block_sem, first_sem, send_sem, recv_sem,
):
    steps, rows = blocks.shape[0], blocks.shape[1]
    group, _, reverse, _, _ = ring_place(cycle, replicas)
    size = rows // pieces
    layer_id, lane = group // LANES, lax.rem(group, LANES)
    pair, core = lane // 2, lax.rem(lane, 2)
    along = LANES * (1 - 2 * reverse)
    ahead = lax.rem(group + along + cycle, cycle)
    behind = lax.rem(group - along + cycle, cycle)
    across = layer_id * LANES + (1 - pair) * 2 + core
    beside = layer_id * LANES + pair * 2 + 1 - core
    lane_across = (1 - pair) * 2 + core
    first = pltpu.make_async_copy(features, slots.at[0, lane], first_sem)
    first.start()

    def load(step):
        return pltpu.make_async_copy(
            dense.at[step], blocks.at[step], block_sem.at[step]
        )

    def in_order(hop):
        return hop * (1 - reverse) + (steps - 1 - hop) * reverse

    @pl.loop(0, steps)
    def _(hop):
        load(in_order(hop)).start()

    greet((ahead, behind, across, beside))
    first.wait()

    def copy(kind, distance, piece):
        span = pl.ds(piece * size, size)
        whose = lane_across if kind == RELAYED else lane
        landing = distance + 1 if kind == OVER_LAYERS else distance
        return pltpu.make_async_remote_copy(
            src_ref=slots.at[distance, whose, span],
            dst_ref=slots.at[landing, whose, span],
            send_sem=send_sem.at[kind, distance, piece],
            recv_sem=recv_sem.at[kind, distance, piece],
            device_id={"blk": {OVER_LAYERS: ahead, OVER_PAIR: across}.get(kind, beside)},
            device_id_type=pl.DeviceIdType.MESH,
        )

    def gives(distance):
        return {0: pair == reverse, 1: None, 2: pair != reverse}[distance]

    def gets(distance):
        return {0: pair != reverse, 1: None, 2: pair == reverse}[distance]

    def guarded(condition, act):
        if condition is None:
            act()
        else:
            pl.when(condition)(act)

    def give(distance, piece):
        if distance < 2:
            copy(OVER_LAYERS, distance, piece).start()
        guarded(gives(distance), lambda: copy(OVER_PAIR, distance, piece).start())
        copy(OVER_CORE, distance, piece).start()

    def relay(distance):
        def act():
            for piece in range(pieces):
                copy(OVER_PAIR, distance, piece).wait_recv()
                copy(RELAYED, distance, piece).start()

        guarded(gets(distance), act)

    def arrive(distance):
        for piece in range(pieces):
            copy(OVER_LAYERS, distance - 1, piece).wait_recv()
            give(distance, piece)

    def multiply(distance):
        for piece in range(pieces):
            copy(OVER_CORE, distance, piece).wait_recv()

        def act():
            for piece in range(pieces):
                copy(RELAYED, distance, piece).wait_recv()

        guarded(gets(distance), act)

        @pl.loop(0, steps)
        def _(hop):
            step = in_order(hop)
            away = hop + reverse
            source = lax.rem(lane + (2 * reverse - 1) * away + 2 * steps, LANES)
            far = ((LANES - 1 - lane) * (1 - reverse) + lane * reverse + away) // LANES

            @pl.when(far == distance)
            def _():
                load(step).wait()
                total[...] += jnp.dot(
                    blocks[step], slots[distance, source],
                    preferred_element_type=jnp.float32,
                )

    for piece in range(pieces):
        give(0, piece)
    total[...] = jnp.zeros_like(total)
    arrive(1)
    relay(0)
    multiply(0)
    relay(1)
    arrive(2)
    multiply(1)
    relay(2)
    multiply(2)
    out[...] = total[...].astype(out.dtype)
    for distance in range(3):
        for piece in range(pieces):
            if distance < 2:
                copy(OVER_LAYERS, distance, piece).wait_send()
            guarded(
                gives(distance),
                functools.partial(copy(OVER_PAIR, distance, piece).wait_send),
            )
            copy(OVER_CORE, distance, piece).wait_send()
            guarded(
                gets(distance),
                functools.partial(copy(RELAYED, distance, piece).wait_send),
            )


def forward(cycle, replicas, features, dense):
    step_count, row_total, _ = dense.shape
    width = features.shape[1]
    pieces = 4
    layered = step_count == 2 * LANES and cycle >= 3 * LANES and replicas == 2
    if layered:
        slots, sems = (3, LANES, row_total, width), (4, 3, pieces)
    else:
        slots, sems = (step_count + 1, row_total, width), (step_count, pieces)
    return pl.pallas_call(
        functools.partial(
            layered_forward_kernel if layered else forward_kernel,
            cycle, replicas, pieces,
        ),
        in_specs=[pl.BlockSpec(memory_space=pl.ANY)] * 2,
        out_specs=pl.BlockSpec(memory_space=pltpu.VMEM),
        out_shape=jax.ShapeDtypeStruct((row_total, width), jnp.bfloat16),
        scratch_shapes=[
            pltpu.VMEM(slots, jnp.bfloat16),
            pltpu.VMEM(dense.shape, jnp.bfloat16),
            pltpu.VMEM((row_total, width), jnp.float32),
            pltpu.SemaphoreType.DMA((step_count,)),
            pltpu.SemaphoreType.DMA,
            pltpu.SemaphoreType.DMA(sems),
            pltpu.SemaphoreType.DMA(sems),
        ],
        compiler_params=pltpu.CompilerParams(collective_id=0, has_side_effects=True),
        name="forward",
    )(features, dense)


def layer_kernel(
    features, mine, other, weight_self, weight_neighbor, bias, cotangent,
    activations, sent_t, self_t, grads,
):
    f32 = jnp.float32
    width = features.shape[1]
    aggregate = (mine[...].astype(f32) + other[...].astype(f32)).astype(jnp.bfloat16)
    pre = (
        jnp.dot(features[...], weight_self[...], preferred_element_type=f32)
        + jnp.dot(aggregate, weight_neighbor[...], preferred_element_type=f32)
        + bias[...]
    )
    sigmoid = jax.nn.sigmoid(pre)
    activations[...] = (pre * sigmoid).astype(activations.dtype)
    derivative = sigmoid * (1.0 + pre * (1.0 - sigmoid))
    grad_pre = (cotangent[...].astype(f32) * derivative).astype(jnp.bfloat16)
    sent_t[...] = lax.dot_general(
        weight_neighbor[...], grad_pre, COLS_COLS, preferred_element_type=f32
    ).astype(sent_t.dtype)
    self_t[...] = lax.dot_general(
        weight_self[...], grad_pre, COLS_COLS, preferred_element_type=f32
    )
    grad_self = lax.dot_general(
        features[...], grad_pre, ROWS_ROWS, preferred_element_type=f32
    ).astype(grads.dtype)
    grad_neighbor = lax.dot_general(
        aggregate, grad_pre, ROWS_ROWS, preferred_element_type=f32
    ).astype(grads.dtype)
    summed = jnp.sum(grad_pre.astype(f32), axis=0, keepdims=True)
    parts = grads.shape[0]
    depth = 2 * width // parts
    tail = grads.shape[1] - depth
    bias_rows = jnp.broadcast_to(summed, (tail, width)).astype(grads.dtype)
    for part in range(parts):
        source, place = (
            (grad_self, part) if 2 * part < parts else (grad_neighbor, part - parts // 2)
        )
        grads[part, 0:depth, :] = source[place * depth : (place + 1) * depth, :]
        grads[part, depth:, :] = bias_rows


def layer(parts, features, mine, other, weight_self, weight_neighbor, bias, cotangent):
    row_total, width = features.shape
    shape = jax.ShapeDtypeStruct
    return pl.pallas_call(
        layer_kernel,
        out_shape=(
            shape((row_total, width), jnp.bfloat16),
            shape((width, row_total), jnp.bfloat16),
            shape((width, row_total), jnp.float32),
            shape((parts, 2 * width // parts + 16, width), jnp.bfloat16),
        ),
        name="layer",
    )(features, mine, other, weight_self, weight_neighbor, bias, cotangent)


def backward_kernel(
    cycle, replicas, pieces, sent_t, dense, grads, out, part_out,
    landed, held, part_landed, part_held, blocks, term,
    block_sem, send_sem, recv_sem,
):
    steps = blocks.shape[0]
    width = sent_t.shape[0]
    size = width // pieces
    f32 = jnp.float32
    group, replica, reverse, behind, ahead = ring_place(cycle, replicas)

    def load(step):
        return pltpu.make_async_copy(
            dense.at[step], blocks.at[step], block_sem.at[step]
        )

    def in_order(hop):
        return (steps - 1 - hop) * (1 - reverse) + hop * reverse

    @pl.loop(0, steps)
    def _(hop):
        load(in_order(hop)).start()

    greet((ahead, behind))

    def hop_copy(hop, piece):
        if piece < pieces:
            span = pl.ds(piece * size, size)
            source, target = held.at[hop, span], landed.at[hop, span]
        else:
            source, target = part_held.at[hop], part_landed.at[hop]
        return pltpu.make_async_remote_copy(
            src_ref=source,
            dst_ref=target,
            send_sem=send_sem.at[hop, piece],
            recv_sem=recv_sem.at[hop, piece],
            device_id={"blk": ahead},
            device_id_type=pl.DeviceIdType.MESH,
        )

    hops = steps - 1 + reverse

    @pl.loop(0, steps)
    def _(hop):
        step = in_order(hop)
        target = lax.rem(group - steps * replica - step + 2 * cycle, cycle)
        load(step).wait()
        term[...] = jnp.dot(sent_t[...], blocks[step], preferred_element_type=f32)
        for piece in range(pieces + 1):
            span = pl.ds(piece * size, size)

            @pl.when(hop > 0)
            def _():
                hop_copy(hop - 1, piece).wait_recv()
                if piece < pieces:
                    held[hop, span] = (
                        term[span] + landed[hop - 1, span].astype(f32)
                    ).astype(held.dtype)
                else:
                    part_held[hop] = (
                        grads[target].astype(f32) + part_landed[hop - 1].astype(f32)
                    ).astype(part_held.dtype)

            @pl.when(hop == 0)
            def _():
                if piece < pieces:
                    held[hop, span] = term[span].astype(held.dtype)
                else:
                    part_held[hop] = grads[target]

            @pl.when(hop < hops)
            def _():
                hop_copy(hop, piece).start()

    @pl.when(reverse == 0)
    def _():
        out[...] = held[steps - 1]
        part_out[...] = part_held[steps - 1]

    @pl.when(reverse == 1)
    def _():
        for piece in range(pieces + 1):
            hop_copy(steps - 1, piece).wait_recv()
        out[...] = landed[steps - 1]
        part_out[...] = part_landed[steps - 1]

    @pl.loop(0, hops)
    def _(hop):
        for piece in range(pieces + 1):
            hop_copy(hop, piece).wait_send()


def backward(cycle, replicas, sent_t, dense, grads):
    step_count, row_total, _ = dense.shape
    width = sent_t.shape[0]
    part = grads.shape[1:]
    pieces = 4
    bf16 = jnp.bfloat16
    return pl.pallas_call(
        functools.partial(backward_kernel, cycle, replicas, pieces),
        in_specs=[
            pl.BlockSpec(memory_space=pltpu.VMEM),
            pl.BlockSpec(memory_space=pl.ANY),
            pl.BlockSpec(memory_space=pltpu.VMEM),
        ],
        out_specs=[pl.BlockSpec(memory_space=pltpu.VMEM)] * 2,
        out_shape=(
            jax.ShapeDtypeStruct((width, row_total), bf16),
            jax.ShapeDtypeStruct(part, bf16),
        ),
        scratch_shapes=[
            pltpu.VMEM((step_count, width, row_total), bf16),
            pltpu.VMEM((step_count, width, row_total), bf16),
            pltpu.VMEM((step_count, *part), bf16),
            pltpu.VMEM((step_count, *part), bf16),
            pltpu.VMEM(dense.shape, bf16),
            pltpu.VMEM((width, row_total), jnp.float32),
            pltpu.SemaphoreType.DMA((step_count,)),
            pltpu.SemaphoreType.DMA((step_count, pieces + 1)),
            pltpu.SemaphoreType.DMA((step_count, pieces + 1)),
        ],
        compiler_params=pltpu.CompilerParams(collective_id=1, has_side_effects=True),
        name="backward",
    )(sent_t, dense, grads)


def finish_kernel(
    cycle, replicas, pushed, part, self_t, weights, bias_out, grad_t,
    gathered, landed, part_landed, pair_send, pair_recv, send_sem, recv_sem,
):
    f32 = jnp.float32
    depth = gathered.shape[1]
    group = lax.axis_index("blk")
    partner = {"rep": lax.rem(lax.axis_index("rep") + replicas // 2, replicas)}
    mesh_id = pl.DeviceIdType.MESH
    barrier = pltpu.get_barrier_semaphore()
    pl.semaphore_signal(barrier, inc=1, device_id=partner, device_id_type=mesh_id)
    for away in range(1, cycle):
        pl.semaphore_signal(
            barrier, inc=1, device_id={"blk": lax.rem(group + away, cycle)},
            device_id_type=mesh_id,
        )
    pl.semaphore_wait(barrier, cycle)

    def swap(source, target, index):
        return pltpu.make_async_remote_copy(
            src_ref=source, dst_ref=target,
            send_sem=pair_send.at[index], recv_sem=pair_recv.at[index],
            device_id=partner, device_id_type=mesh_id,
        )

    part_swap = swap(part, part_landed, 0)
    part_swap.start()
    panel_swap = swap(pushed, landed, 1)
    panel_swap.start()
    part_swap.wait()
    summed = part[...].astype(f32) + part_landed[...].astype(f32)
    bias_out[...] = summed[depth:]
    gathered[group] = summed[:depth].astype(gathered.dtype)

    def put(away):
        return pltpu.make_async_remote_copy(
            src_ref=gathered.at[group],
            dst_ref=gathered.at[group],
            send_sem=send_sem.at[away],
            recv_sem=recv_sem.at[away],
            device_id={"blk": lax.rem(group + away, cycle)},
            device_id_type=mesh_id,
        )

    @pl.loop(1, cycle)
    def _(away):
        put(away).start()

    @pl.loop(1, cycle)
    def _(away):
        put(away).wait()

    weights[...] = gathered[...].astype(f32)
    panel_swap.wait()
    grad_t[...] = (
        self_t[...] + (pushed[...].astype(f32) + landed[...].astype(f32))
    ).astype(grad_t.dtype)


def finish(cycle, replicas, pushed, part, self_t):
    width = pushed.shape[0]
    depth = 2 * width // cycle
    tail = part.shape[0] - depth
    shape = jax.ShapeDtypeStruct
    return pl.pallas_call(
        functools.partial(finish_kernel, cycle, replicas),
        in_specs=[pl.BlockSpec(memory_space=pltpu.VMEM)] * 3,
        out_specs=[pl.BlockSpec(memory_space=pltpu.VMEM)] * 3,
        out_shape=(
            shape((cycle, depth, width), jnp.float32),
            shape((tail, width), jnp.float32),
            shape(pushed.shape, jnp.bfloat16),
        ),
        scratch_shapes=[
            pltpu.VMEM((cycle, depth, width), jnp.bfloat16),
            pltpu.VMEM(pushed.shape, jnp.bfloat16),
            pltpu.VMEM(part.shape, jnp.bfloat16),
            pltpu.SemaphoreType.DMA((2,)),
            pltpu.SemaphoreType.DMA((2,)),
            pltpu.SemaphoreType.DMA((cycle,)),
            pltpu.SemaphoreType.DMA((cycle,)),
        ],
        compiler_params=pltpu.CompilerParams(collective_id=2, has_side_effects=True),
        name="finish",
    )(pushed, part, self_t)


def on_device(
    features,
    weight_self,
    weight_neighbor,
    bias_vector,
    tile_row,
    tile_column,
    tile_value,
    tile_count,
    tile_table,
    cotangent,
):
    f32, bf16 = jnp.float32, jnp.bfloat16
    cycle_length = lax.axis_size("blk")
    replicas = lax.axis_size("rep")
    step_count = cycle_length // replicas
    replica = lax.axis_index("rep")
    row_total, width = features.shape

    jump = jnp.minimum(replica, replicas - 1 - replica)
    jump_bits = max(replicas // 2 - 1, 0).bit_length()
    reverse = (2 * replica) // replicas

    def shifted(array, sign):
        for bit in range(jump_bits):
            by = sign * (step_count << bit)
            moved = jnp.where(
                reverse == 0,
                lax.ppermute(
                    array, "blk",
                    [(i, (i + by) % cycle_length) for i in range(cycle_length)],
                ),
                lax.ppermute(
                    array, "blk",
                    [(i, (i - by) % cycle_length) for i in range(cycle_length)],
                ),
            )
            array = jnp.where(jump // (1 << bit) % 2 == 1, moved, array)
        return array

    dense = build_dense(
        tile_row[0], tile_column[0], tile_value[0], tile_count[0], tile_table, row_total
    )
    mine = forward(cycle_length, replicas, shifted(features, 1), dense)
    bit = 1
    while True:
        other = lax.ppermute(mine, "rep", [(i, i ^ bit) for i in range(replicas)])
        bit *= 2
        if bit >= replicas:
            break
        mine = (mine.astype(f32) + other.astype(f32)).astype(bf16)
    activations, sent_t, self_t, grads = layer(
        cycle_length, features, mine, other, weight_self, weight_neighbor,
        bias_vector.reshape(1, width), cotangent,
    )
    pushed, part = backward(cycle_length, replicas, sent_t, dense, grads)
    pushed, part = shifted(pushed, -1), shifted(part, -1)

    def over_replicas(array):
        bit = 1
        while 2 * bit < replicas:
            other = lax.ppermute(array, "rep", [(i, i ^ bit) for i in range(replicas)])
            array = (array.astype(f32) + other.astype(f32)).astype(bf16)
            bit *= 2
        return array

    weights, bias_rows, grad_t = finish(
        cycle_length, replicas, over_replicas(pushed), over_replicas(part), self_t
    )
    weights = weights.reshape(2 * width, width)
    grad_features = grad_t.T
    return (
        activations,
        grad_features,
        weights[:width],
        weights[width:],
        bias_rows[0],
    )


def solution(mesh):
    placed = (
        P("blk", None),
        P(),
        P(),
        P(),
        P("blk", "rep", None),
        P("blk", "rep", None),
        P("blk", "rep", None),
        P("blk", "rep"),
        P(("blk", "rep"), None, None),
        P("blk", None),
    )
    return jax.shard_map(
        on_device,
        mesh=mesh,
        in_specs=placed,
        out_specs=(P("blk", None), P("blk", None), P(), P(), P()),
        check_vma=False,
    )
```
